32 devices in a mesh: parts: 2 (over y), ctx: 4 (over z), head: 2 (over x), rep: 2 (over core).
Axes of the slice: x: 2, y: 2, z: 4, core: 2. Of those that a mesh axis runs over, the one named last changes fastest.
Arguments:
- query_rows: bfloat16 [4096, 8, 6, 128], P(('parts', 'ctx'), 'head', 'rep'), parts along dimension 0, may hold values from -125 to 125
- key_rows: bfloat16 [4096, 8, 128], P(('parts', 'ctx'), 'head'), parts along dimension 0, may hold values from -5 to 5
- value_rows: bfloat16 [4096, 8, 128], P(('parts', 'ctx'), 'head'), parts along dimension 0, may hold values from -6 to 6
- dest_block: int32 [32], P('parts'), parts along dimension 0, may hold values from 0 to 15, as said below
- tile_list: int32 [32, 4], P('parts'), parts along dimension 0, may hold values from 0 to 15, as said below
- tile_count: int32 [32], P('parts'), parts along dimension 0, may hold values from 1 to 4
- stripe_start: int32 [16, 4], P(('parts', 'head')), parts along dimension 0, may hold values from 0 to 1536, as said below
Outputs:
- attended: bfloat16 [4096, 8, 6, 128], P(('parts', 'ctx'), 'head', 'rep'), parts along dimension 0
The draws below stay inside these ranges and needn't reach their ends.
There are 2 independent parts, one for each index of `parts`. The reference program is written for one: setup_inputs(seed, part) draws one part's arguments, and reference() takes and returns one part's arrays. A program takes and returns all parts, laid end to end along the dimension named above; each array names one. Nothing has to cross between parts.
Inputs may be any that keep to these rules, and one draw needn't show every extreme that they name: dest_block is a permutation of the blocks, so each index of ctx receives exactly 4 blocks (index of ctx of a position: dest_block // 4). For every ordered pair of indices of ctx, at most 1 of the first index's blocks take positions on the second, and some pair has exactly 1. tile_list[p, 0] == p; the 4 tiles of a row are distinct and all on the same index of ctx as p (tile_list[p, j] // 4 == p // 4). Each stripe lies in the rows of one index of ctx: stripe_start // 512 == (stripe_start + 511) // 512 (since a stripe is 512 keys long, stripe_start is a multiple of 512).
All inputs are finite; a program needn't handle non-finite values.
Results may differ from the reference program's by a relative error of at most 0.0048.
Values may be sent and summed in bfloat16 or wider, within the bound.
No kernel may reach another device: no remote copies, remote signals or barrier semaphores. Data moves between devices by JAX's collectives and lax.ppermute only.
A program may use at most 64 MiB of HBM per device.

```python
import jax
import jax.numpy as jnp
from jax import lax

HD = 128
KVH = 8
GROUP = 6
TOK_DEV = 512
LT = 4
NSTRIPE = 4
STRIPE = 512
LENGTH = 2048
BPD = 4
NBLK = 16


def shared_rows(key):
    key_draw = jnp.clip(jax.random.normal(jax.random.fold_in(key, 21), (LENGTH, KVH, HD), jnp.float32), -5.0, 5.0)
    query_draw = jnp.clip(jax.random.normal(jax.random.fold_in(key, 22), (LENGTH, KVH, GROUP, HD), jnp.float32), -5.0, 5.0)
    return (query_draw, key_draw)


def draw_query_rows(key, part):
    return shared_rows(key)[0].astype(jnp.bfloat16)


def draw_key_rows(key, part):
    return shared_rows(key)[1].astype(jnp.bfloat16)


def draw_dest_block(key, part):
    device_total = NBLK // BPD
    device_map = jax.random.permutation(jax.random.fold_in(key, 31), device_total)
    source_map = jax.random.permutation(jax.random.fold_in(key, 32), device_total)
    rotation = jax.random.permutation(jax.random.fold_in(key, 33), device_total)
    shifts = jax.random.randint(jax.random.fold_in(key, 34), (device_total,), 0, BPD)
    block_ids = jnp.arange(NBLK)
    source = block_ids // BPD
    local_slot = (block_ids % BPD + shifts[source]) % BPD
    target = device_map[(source_map[source] + rotation[local_slot % device_total]) % device_total]
    jitter = jax.random.permutation(jax.random.fold_in(key, 35), NBLK)
    scores = target * NBLK + jitter
    ordering = jnp.argsort(scores)
    return jnp.argsort(ordering).astype(jnp.int32)


def draw_tile_list(key, part):
    block_ids = jnp.arange(NBLK)
    raw = jax.random.randint(jax.random.fold_in(key, 41), (NBLK, BPD), 0, 1 << 20)
    scores = raw * BPD + jnp.arange(BPD)[None, :] + 1
    own_column = (block_ids % BPD)[:, None] == jnp.arange(BPD)[None, :]
    scores = jnp.where(own_column, 0, scores)
    ordering = jnp.argsort(scores, axis=1)[:, :LT]
    return ((block_ids // BPD)[:, None] * BPD + ordering).astype(jnp.int32)


def draw_tile_count(key, part):
    counts = jax.random.randint(jax.random.fold_in(key, 51), (NBLK,), 1, LT + 1)
    return jnp.where(jnp.arange(NBLK) == 0, LT, counts).astype(jnp.int32)


def draw_stripe_start(key, part):
    device_total = NBLK // BPD
    owners = jax.random.randint(jax.random.fold_in(key, 61), (KVH, NSTRIPE), 0, device_total)
    offsets = jax.random.randint(jax.random.fold_in(key, 62), (KVH, NSTRIPE), 0, TOK_DEV - STRIPE + 1)
    starts = owners * TOK_DEV + offsets
    corner = (jnp.arange(KVH)[:, None] == 0) & (jnp.arange(NSTRIPE)[None, :] == NSTRIPE - 1)
    return jnp.where(corner, LENGTH - STRIPE, starts).astype(jnp.int32)


def levels(own_key, extent, split, least, high):
    gain = 1.0
    for dim, parts in split:
        draws = jax.random.uniform(jax.random.fold_in(jax.random.fold_in(own_key, 6), dim), (parts,), jnp.float32, least / len(split), high / len(split))
        gain = gain * jnp.repeat(jnp.exp(draws), extent[dim] // parts).reshape((-1,) + (1,) * (len(extent) - 1 - dim))
    return gain


def gaussian(stream_key, dims, width, limit, split=(), kind=jnp.bfloat16):
    loudness = levels(stream_key, dims, split, -0.22, 0.18) if split else 1.0
    values = jax.random.normal(stream_key, dims, jnp.float32) * width * loudness
    return jnp.minimum(jnp.maximum(values, -limit), limit).astype(kind)


def setup_inputs(seed: int = 0, part: int = 0) -> dict:
    arg_keys = jax.random.split(jax.random.key(seed), 8)
    part_keys = jax.random.split(jax.random.fold_in(arg_keys[7], part), 8)
    return {
        "query_rows": draw_query_rows(jax.random.fold_in(jax.random.fold_in(arg_keys[7], part), 71), part),
        "key_rows": draw_key_rows(jax.random.fold_in(jax.random.fold_in(arg_keys[7], part), 71), part),
        "value_rows": gaussian(part_keys[2], (LENGTH, KVH, HD), 1.0, 6.0, ((0, 4), (1, 2))),
        "dest_block": draw_dest_block(jax.random.fold_in(jax.random.fold_in(arg_keys[7], part), 71), part),
        "tile_list": draw_tile_list(jax.random.fold_in(jax.random.fold_in(arg_keys[7], part), 71), part),
        "tile_count": draw_tile_count(jax.random.fold_in(jax.random.fold_in(arg_keys[7], part), 71), part),
        "stripe_start": draw_stripe_start(jax.random.fold_in(jax.random.fold_in(arg_keys[7], part), 71), part),
    }


def attend(query_block, tile_key, tile_value, tile_used, stripe_keys, stripe_values):
    scaling = query_block.shape[-1] ** -0.5
    block_rows = query_block.shape[0]
    query_wide = query_block.astype(jnp.float32)
    near_scores = jnp.einsum("qhgd,khd->hgqk", query_wide, tile_key.astype(jnp.float32)) * scaling
    far_scores = jnp.einsum("qhgd,hkd->hgqk", query_wide, stripe_keys.astype(jnp.float32)) * scaling
    kept_mask = jnp.arange(near_scores.shape[-1], dtype=jnp.int32) // block_rows < tile_used
    near_scores = jnp.where(kept_mask, near_scores, -1e30)
    row_top = jnp.maximum(jnp.max(near_scores, axis=-1), jnp.max(far_scores, axis=-1))[..., None]
    near_weight = jnp.exp(near_scores - row_top)
    far_weight = jnp.exp(far_scores - row_top)
    denominator = jnp.sum(near_weight, axis=-1) + jnp.sum(far_weight, axis=-1)
    near_rounded = lax.optimization_barrier(near_weight.astype(jnp.bfloat16)).astype(jnp.float32)
    far_rounded = lax.optimization_barrier(far_weight.astype(jnp.bfloat16)).astype(jnp.float32)
    summed = jnp.einsum("hgqk,khd->qhgd", near_rounded, tile_value.astype(jnp.float32))
    summed = summed + jnp.einsum("hgqk,hkd->qhgd", far_rounded, stripe_values.astype(jnp.float32))
    return (summed / jnp.transpose(denominator, (2, 0, 1))[..., None]).astype(jnp.bfloat16)


def reference(query_rows, key_rows, value_rows, dest_block, tile_list, tile_count, stripe_start):
    block_total = dest_block.shape[0]
    block_rows = query_rows.shape[0] // block_total
    inverse = jnp.zeros((block_total,), jnp.int32).at[dest_block].set(jnp.arange(block_total, dtype=jnp.int32))
    query_new = query_rows.reshape(block_total, block_rows, KVH, GROUP, HD)[inverse]
    key_new = key_rows.reshape(block_total, block_rows, KVH, HD)[inverse]
    value_new = value_rows.reshape(block_total, block_rows, KVH, HD)[inverse]
    stripe_span = jnp.arange(STRIPE, dtype=jnp.int32)
    stripe_rows = (stripe_start[:, :, None] + stripe_span[None, None, :]).reshape(KVH, NSTRIPE * STRIPE)
    head_index = jnp.arange(KVH, dtype=jnp.int32)[:, None]
    stripe_keys = key_new.reshape(block_total * block_rows, KVH, HD)[stripe_rows, head_index]
    stripe_values = value_new.reshape(block_total * block_rows, KVH, HD)[stripe_rows, head_index]

    def attend_block(packed):
        query_block, tile_ids, tile_used = packed
        tile_key = key_new[tile_ids].reshape(LT * block_rows, KVH, HD)
        tile_value = value_new[tile_ids].reshape(LT * block_rows, KVH, HD)
        return attend(query_block, tile_key, tile_value, tile_used, stripe_keys, stripe_values)

    out_new = lax.map(attend_block, (query_new, tile_list, tile_count))
    return out_new[dest_block].reshape(query_rows.shape)
```

```python
import functools
import math

import jax
import jax.numpy as jnp
from jax import lax
from jax.experimental import pallas as pl
from jax.experimental.pallas import tpu as pltpu
from jax.sharding import PartitionSpec as P

NEG = -1e30


def attend_kernel(slots, first, last, scale, *refs):
    src_ref, bias_ref, q_ref = refs[:3]
    kv_refs = refs[3 : 3 + 2 * slots]
    rest = refs[3 + 2 * slots :]
    if first:
        acc_in, top_in = None, None
        outs = rest
    else:
        acc_in, top_in = rest[:2]
        outs = rest[2:]
    pairs, rows, width = q_ref.shape
    heads = kv_refs[0].shape[1]
    half = kv_refs[0].shape[2]
    blocks = pairs // heads
    block_rows = half * 2 // blocks
    half_blocks = half // block_rows
    rep = src_ref[0]
    ones = jnp.ones((half, width), jnp.bfloat16)

    def update(pair, slot, acc_src, top_src, acc_dst, top_dst, fresh):
        head = pair // blocks
        source = src_ref[1 + slot]
        query = q_ref[pair]
        scores = []
        for part in range(2):
            ref = kv_refs[2 * slot + part]
            raw = lax.dot_general(
                query, ref[0, head], (((1,), (1,)), ((), ())), preferred_element_type=jnp.float32
            )
            base = source * blocks + (rep if part == 0 else 1 - rep) * half_blocks
            for piece in range(half_blocks):
                cut = raw[:, piece * block_rows : (piece + 1) * block_rows]
                scores.append(cut * scale + bias_ref[pair, base + piece])
        top = functools.reduce(jnp.maximum, scores)
        top = jnp.max(top, axis=-1, keepdims=True)
        if not fresh:
            before = top_src[pair][:, :1]
            top = jnp.maximum(top, before)
        weights = [jnp.exp2(piece - top).astype(jnp.bfloat16) for piece in scores]
        total = None
        for part in range(2):
            ref = kv_refs[2 * slot + part]
            value = jnp.concatenate([ref[1, head], ones], axis=1)
            weight = jnp.concatenate(
                weights[part * half_blocks : (part + 1) * half_blocks], axis=1
            )
            term = jnp.dot(weight, value, preferred_element_type=jnp.float32)
            total = term if total is None else total + term
        if not fresh:
            total = total + acc_src[pair] * jnp.exp2(before - top)
        acc_dst[pair] = total
        top_dst[pair] = jnp.broadcast_to(top, top_dst.shape[1:])

    if first:
        acc_dst, top_dst = outs[:2]
    elif last:
        acc_dst, top_dst = outs[1:3]
    else:
        acc_dst, top_dst = outs[:2]

    if first:
        @pl.loop(0, pairs)
        def _(pair):
            update(pair, 0, None, None, acc_dst, top_dst, True)
    else:

        @pl.loop(0, pairs)
        def _(pair):
            acc_dst[pair] = acc_in[pair]
            top_dst[pair] = top_in[pair]

        for slot in range(slots):

            @pl.when(src_ref[1 + slot] >= 0)
            def _():
                @pl.loop(0, pairs)
                def _(pair):
                    update(pair, slot, acc_dst, top_dst, acc_dst, top_dst, False)
    if last:
        out_ref = outs[0]

        @pl.loop(0, pairs)
        def _(pair):
            total = acc_dst[pair]
            out_ref[pair] = (total[:, :width] / total[:, width:]).astype(out_ref.dtype)


def attend_call(sources, bias, query, kv, state, last, scale):
    pairs, rows, width = query.shape
    slots = len(kv) // 2
    first = state is None
    vmem = pl.BlockSpec(memory_space=pltpu.VMEM)
    smem = pl.BlockSpec(memory_space=pltpu.SMEM)
    operands = [sources, bias, query, *kv]
    specs = [smem, smem] + [vmem] * (1 + len(kv))
    shapes = [
        jax.ShapeDtypeStruct((pairs, rows, 2 * width), jnp.float32),
        jax.ShapeDtypeStruct((pairs, rows, width), jnp.float32),
    ]
    aliases = {}
    if not first:
        aliases = {len(operands): 0, len(operands) + 1: 1}
        operands += list(state)
        specs += [vmem, vmem]
    if last:
        shapes = [jax.ShapeDtypeStruct((pairs, rows, width), jnp.bfloat16)] + shapes
        aliases = {key: value + 1 for key, value in aliases.items()}
    keys = slots * 2 * kv[0].shape[2]
    work = pairs * rows * keys
    return pl.pallas_call(
        functools.partial(attend_kernel, slots, first, last, scale),
        out_shape=shapes,
        in_specs=specs,
        out_specs=[vmem] * len(shapes),
        input_output_aliases=aliases,
        compiler_params=pltpu.CompilerParams(vmem_limit_bytes=40 << 20),
        cost_estimate=pl.CostEstimate(
            flops=6 * work * width, bytes_accessed=4 * pairs * rows * width, transcendentals=work
        ),
    )(*operands)


def local(query_rows, key_rows, value_rows, dest_block, tile_list, tile_count, stripe_start):
    ctx_count = lax.axis_size("ctx")
    ctx_index = lax.axis_index("ctx")
    rep_index = lax.axis_index("rep")
    tok_rows, heads, group, width = query_rows.shape
    block_total = dest_block.shape[0]
    blocks = block_total // ctx_count
    block_rows = tok_rows // blocks
    half = tok_rows // 2
    scale = width ** (-0.5) * math.log2(math.e)

    def half_of(which):
        key_half = lax.dynamic_slice_in_dim(key_rows, which * half, half, 0)
        value_half = lax.dynamic_slice_in_dim(value_rows, which * half, half, 0)
        return jnp.transpose(jnp.stack([key_half, value_half]), (0, 2, 1, 3))

    def swap(array):
        return lax.ppermute(array, "rep", [(0, 1), (1, 0)])

    mine = half_of(rep_index)
    right = [(i, i + 1) for i in range(ctx_count - 1)]
    left = [(i + 1, i) for i in range(ctx_count - 1)]
    steps = []
    from_left, from_right = mine, mine
    for hop in range(1, max(2, ctx_count - 1)):
        if ctx_count == 1:
            break
        from_left = lax.ppermute(from_left, "ctx", right)
        from_right = lax.ppermute(from_right, "ctx", left)
        steps.append(
            (
                (from_left, from_right),
                (ctx_index - hop, jnp.where(ctx_index + hop < ctx_count, ctx_index + hop, -1)),
            )
        )
        if hop == 1 and ctx_count > 2:
            far = lax.ppermute(mine, "ctx", [(0, ctx_count - 1), (ctx_count - 1, 0)])
            far_source = jnp.where(
                ctx_index == 0, ctx_count - 1, jnp.where(ctx_index == ctx_count - 1, 0, -1)
            )
            steps.append(((far,), (far_source,)))

    owner = dest_block // blocks
    stripes = jnp.sum(
        (stripe_start[:, :, None] // tok_rows == owner[None, None, :]).astype(jnp.int32), axis=1
    )
    placed = lax.dynamic_slice_in_dim(dest_block, ctx_index * blocks, blocks, 0)
    row_pick = (placed[:, None] == jnp.arange(block_total)[None, :]).astype(jnp.int32)
    used = jnp.arange(tile_list.shape[1])[None, :] < tile_count[:, None]
    listed = jnp.sum(
        (used[:, :, None] & (tile_list[:, :, None] == dest_block[None, None, :])).astype(jnp.int32),
        axis=1,
    )
    near = jnp.sum(row_pick[:, :, None] * listed[None], axis=1)
    count = stripes[:, None, :] + near[None, :, :]
    bias = jnp.where(count > 0, jnp.log2(jnp.maximum(count, 1).astype(jnp.float32)), NEG)
    bias = bias.reshape(heads * blocks, block_total)

    query = query_rows.reshape(blocks, block_rows, heads, group, width)
    query = jnp.transpose(query, (2, 0, 3, 1, 4)).reshape(
        heads * blocks, group * block_rows, width
    )

    def scalars(values):
        return jnp.stack([rep_index, *values]).astype(jnp.int32)

    state = attend_call(
        scalars((ctx_index,)),
        bias,
        query,
        (mine, half_of(1 - rep_index)),
        None,
        False,
        scale,
    )
    if not steps:
        total = state[0]
        out = (total[..., :width] / total[..., width:]).astype(jnp.bfloat16)
    for index, (arrays, sources) in enumerate(steps):
        kv = []
        for array in arrays:
            kv += [array, swap(array)]
        last = index == len(steps) - 1
        state = attend_call(scalars(sources), bias, query, kv, state, last, scale)
        if last:
            out = state[0]
    out = out.reshape(heads, blocks, group, block_rows, width)
    return jnp.transpose(out, (1, 3, 0, 2, 4)).reshape(query_rows.shape)


def solution(mesh):
    in_specs = (
        P(("parts", "ctx"), "head", "rep", None),
        P(("parts", "ctx"), "head", None),
        P(("parts", "ctx"), "head", None),
        P("parts"),
        P("parts", None),
        P("parts"),
        P(("parts", "head"), None),
    )
    out_specs = P(("parts", "ctx"), "head", "rep", None)
    return jax.shard_map(local, mesh=mesh, in_specs=in_specs, out_specs=out_specs, check_vma=False)
```

```python
import functools
import math

import jax
import jax.numpy as jnp
from jax import lax
from jax.experimental import pallas as pl
from jax.experimental.pallas import tpu as pltpu
from jax.sharding import PartitionSpec as P

NEG = -1e30


ONES = 16
KEEP = 8


def attend_kernel(slots, first, last, scale, *refs):
    src_ref, bias_ref, q_ref = refs[:3]
    kv_refs = refs[3 : 3 + 2 * slots]
    rest = refs[3 + 2 * slots :]
    s_refs = rest[-2:]
    rest = rest[:-2]
    if first:
        acc_in, top_in = None, None
    else:
        acc_in, top_in = rest[:2]
        rest = rest[2:]
    if last:
        out_ref, rest = rest[0], rest[1:]
    acc_out, top_out = rest
    pairs, rows, width = q_ref.shape
    heads = kv_refs[0].shape[1]
    half = kv_refs[0].shape[2]
    blocks = pairs // heads
    block_rows = 2 * half // blocks
    half_blocks = half // block_rows
    rep = src_ref[0]
    ones = jnp.ones((ONES, 2 * half), jnp.bfloat16)

    def score(pair, slot, s_ref):
        head = pair // blocks
        query = q_ref[pair]
        for part in range(2):
            s_ref[part * half : (part + 1) * half] = lax.dot_general(
                kv_refs[2 * slot + part][0, head],
                query,
                (((1,), (1,)), ((), ())),
                preferred_element_type=jnp.float32,
            )

    def absorb(pair, slot, s_ref, acc_src, top_src):
        head = pair // blocks
        source = src_ref[1 + slot]
        offsets, values = [], []
        top = None
        for part in range(2):
            base = source * blocks + (rep if part == 0 else 1 - rep) * half_blocks
            for piece in range(half_blocks):
                start = part * half + piece * block_rows
                offset = bias_ref[pair, base + piece]
                block = s_ref[start : start + block_rows]
                peak = jnp.max(block.reshape(block_rows // 8, 8, rows), axis=0) * scale + offset
                top = peak if top is None else jnp.maximum(top, peak)
                offsets.append(offset)
                values.append(
                    kv_refs[2 * slot + part][1, head, piece * width : (piece + 1) * width, :]
                )
        top = jnp.max(top, axis=0, keepdims=True)
        if acc_src is not None:
            before = top_src[pair, :1]
            top = jnp.maximum(top, before)
        weights = []
        for index, offset in enumerate(offsets):
            block = s_ref[index * block_rows : (index + 1) * block_rows]
            weights.append(jnp.exp2(block * scale - (top - offset)).astype(jnp.bfloat16))
        value = jnp.concatenate([jnp.concatenate(values, axis=1), ones], axis=0)
        term = jnp.dot(
            value, jnp.concatenate(weights, axis=0), preferred_element_type=jnp.float32
        )[: width + KEEP]
        if acc_src is not None:
            term = term + acc_src[pair] * jnp.exp2(before - top)
        acc_out[pair] = term
        top_out[pair] = jnp.broadcast_to(top, top_out.shape[1:])

    def sweep(slot, acc_src, top_src):
        score(0, slot, s_refs[0])

        @pl.loop(0, pairs // 2)
        def _(step):
            pair = 2 * step
            score(pair + 1, slot, s_refs[1])
            absorb(pair, slot, s_refs[0], acc_src, top_src)
            score(jnp.minimum(pair + 2, pairs - 1), slot, s_refs[0])
            absorb(pair + 1, slot, s_refs[1], acc_src, top_src)

    if first:
        sweep(0, None, None)
    else:
        valid = [src_ref[1 + slot] >= 0 for slot in range(slots)]
        seen = None
        for slot in range(slots):
            if seen is None:
                pl.when(valid[slot])(functools.partial(sweep, slot, acc_in, top_in))
                seen = valid[slot]
            else:
                fresh = jnp.logical_and(valid[slot], jnp.logical_not(seen))
                again = jnp.logical_and(valid[slot], seen)
                pl.when(fresh)(functools.partial(sweep, slot, acc_in, top_in))
                pl.when(again)(functools.partial(sweep, slot, acc_out, top_out))
                seen = jnp.logical_or(seen, valid[slot])

        @pl.when(jnp.logical_not(seen))
        def _():
            @pl.loop(0, pairs)
            def _(pair):
                acc_out[pair] = acc_in[pair]
                top_out[pair] = top_in[pair]

    if last:
        row = lax.broadcasted_iota(jnp.int32, (block_rows, block_rows), 0)
        column = lax.broadcasted_iota(jnp.int32, (block_rows, block_rows), 1)
        eye = jnp.where(row == column, 1.0, 0.0).astype(jnp.bfloat16)

        @pl.loop(0, pairs)
        def _(pair):
            total = acc_out[pair]
            value = (total[:width] / total[width : width + 1]).astype(jnp.bfloat16)
            for piece in range(rows // block_rows):
                cut = slice(piece * block_rows, (piece + 1) * block_rows)
                out_ref[pair, cut] = lax.dot_general(
                    eye,
                    value[:, cut],
                    (((1,), (1,)), ((), ())),
                    preferred_element_type=jnp.float32,
                ).astype(out_ref.dtype)


def attend_call(sources, bias, query, kv, state, last, scale):
    pairs, rows, width = query.shape
    slots = len(kv) // 2
    first = state is None
    vmem = pl.BlockSpec(memory_space=pltpu.VMEM)
    smem = pl.BlockSpec(memory_space=pltpu.SMEM)
    operands = [sources, bias, query, *kv]
    specs = [smem, smem] + [vmem] * (1 + len(kv))
    shapes = [
        jax.ShapeDtypeStruct((pairs, width + KEEP, rows), jnp.float32),
        jax.ShapeDtypeStruct((pairs, KEEP, rows), jnp.float32),
    ]
    if not first:
        operands += list(state)
        specs += [vmem, vmem]
    if last:
        shapes = [jax.ShapeDtypeStruct((pairs, rows, width), jnp.bfloat16)] + shapes
    keys = 2 * kv[0].shape[2]
    work = pairs * rows * keys * slots
    return pl.pallas_call(
        functools.partial(attend_kernel, slots, first, last, scale),
        out_shape=shapes,
        in_specs=specs,
        out_specs=[vmem] * len(shapes),
        scratch_shapes=[pltpu.VMEM((keys, rows), jnp.float32)] * 2,
        compiler_params=pltpu.CompilerParams(vmem_limit_bytes=24 << 20),
        cost_estimate=pl.CostEstimate(
            flops=6 * work * width, bytes_accessed=4 * pairs * rows * width, transcendentals=work
        ),
    )(*operands)


def local(query_rows, key_rows, value_rows, dest_block, tile_list, tile_count, stripe_start):
    ctx_count = lax.axis_size("ctx")
    ctx_index = lax.axis_index("ctx")
    rep_index = lax.axis_index("rep")
    tok_rows, heads, group, width = query_rows.shape
    block_total = dest_block.shape[0]
    blocks = block_total // ctx_count
    block_rows = tok_rows // blocks
    half = tok_rows // 2
    scale = width ** (-0.5) * math.log2(math.e)

    def half_of(which):
        key_half = lax.dynamic_slice_in_dim(key_rows, which * half, half, 0)
        value_half = lax.dynamic_slice_in_dim(value_rows, which * half, half, 0)
        key_half = jnp.transpose(key_half, (1, 0, 2))
        value_half = value_half.reshape(half // block_rows, block_rows, heads, width)
        value_half = jnp.transpose(value_half, (2, 0, 3, 1)).reshape(key_half.shape)
        return jnp.stack([key_half, value_half])

    def swap(array):
        return lax.ppermute(array, "rep", [(0, 1), (1, 0)])

    mine = half_of(rep_index)
    right = [(i, i + 1) for i in range(ctx_count - 1)]
    left = [(i + 1, i) for i in range(ctx_count - 1)]
    steps = []
    from_left, from_right = mine, mine
    for hop in range(1, max(2, ctx_count - 1)):
        if ctx_count == 1:
            break
        from_left = lax.ppermute(from_left, "ctx", right)
        from_right = lax.ppermute(from_right, "ctx", left)
        steps.append(
            (
                (from_left, from_right),
                (ctx_index - hop, jnp.where(ctx_index + hop < ctx_count, ctx_index + hop, -1)),
            )
        )
        if hop == 1 and ctx_count > 2:
            far = lax.ppermute(mine, "ctx", [(0, ctx_count - 1), (ctx_count - 1, 0)])
            far_source = jnp.where(
                ctx_index == 0, ctx_count - 1, jnp.where(ctx_index == ctx_count - 1, 0, -1)
            )
            steps.append(((far,), (far_source,)))

    owner = dest_block // blocks
    stripes = jnp.sum(
        (stripe_start[:, :, None] // tok_rows == owner[None, None, :]).astype(jnp.int32), axis=1
    )
    placed = lax.dynamic_slice_in_dim(dest_block, ctx_index * blocks, blocks, 0)
    row_pick = (placed[:, None] == jnp.arange(block_total)[None, :]).astype(jnp.int32)
    used = jnp.arange(tile_list.shape[1])[None, :] < tile_count[:, None]
    listed = jnp.sum(
        (used[:, :, None] & (tile_list[:, :, None] == dest_block[None, None, :])).astype(jnp.int32),
        axis=1,
    )
    near = jnp.sum(row_pick[:, :, None] * listed[None], axis=1)
    count = stripes[:, None, :] + near[None, :, :]
    bias = jnp.where(count > 0, jnp.log2(jnp.maximum(count, 1).astype(jnp.float32)), NEG)
    bias = bias.reshape(heads * blocks, block_total)

    query = query_rows.reshape(blocks, block_rows, heads, group, width)
    query = jnp.transpose(query, (2, 0, 3, 1, 4)).reshape(
        heads * blocks, group * block_rows, width
    )

    def scalars(values):
        return jnp.stack([rep_index, *values]).astype(jnp.int32)

    state = attend_call(
        scalars((ctx_index,)),
        bias,
        query,
        (mine, half_of(1 - rep_index)),
        None,
        False,
        scale,
    )
    if not steps:
        total = state[0]
        out = (total[..., :width] / total[..., width:]).astype(jnp.bfloat16)
    for index, (arrays, sources) in enumerate(steps):
        kv = []
        for array in arrays:
            kv += [array, swap(array)]
        last = index == len(steps) - 1
        state = attend_call(scalars(sources), bias, query, kv, state, last, scale)
        if last:
            out = state[0]
    out = out.reshape(heads, blocks, group, block_rows, width)
    return jnp.transpose(out, (1, 3, 0, 2, 4)).reshape(query_rows.shape)


def solution(mesh):
    in_specs = (
        P(("parts", "ctx"), "head", "rep", None),
        P(("parts", "ctx"), "head", None),
        P(("parts", "ctx"), "head", None),
        P("parts"),
        P("parts", None),
        P("parts"),
        P(("parts", "head"), None),
    )
    out_specs = P(("parts", "ctx"), "head", "rep", None)
    return jax.shard_map(local, mesh=mesh, in_specs=in_specs, out_specs=out_specs, check_vma=False)
```

```python
import functools
import math

import jax
import jax.numpy as jnp
from jax import lax
from jax.experimental import pallas as pl
from jax.experimental.pallas import tpu as pltpu
from jax.sharding import PartitionSpec as P


NEG = -1e30


ONES = 16
KEEP = 8
PACK = 2


def attend_kernel(units, heads, first, last, scale, *refs):
    src_ref, bias_ref, q_ref = refs[:3]
    slots = len(units)
    kv_refs, rest = [], refs[3:]
    for _, parts in units:
        kv_refs.append(rest[: len(parts)])
        rest = rest[len(parts) :]
    s_refs = rest[-2:]
    rest = rest[:-2]
    acc_in, top_in, out_ref, acc_out, top_out = None, None, None, None, None
    if not first:
        acc_in, top_in = rest[:2]
        rest = rest[2:]
    if last:
        out_ref, rest = rest[0], rest[1:]
    acc_out, top_out = rest
    works, rows, width = q_ref.shape
    half = kv_refs[0][0].shape[2]
    blocks = works * PACK // heads
    block_rows = 2 * half // blocks
    half_blocks = half // block_rows
    rep = src_ref[0]

    def score(work, slot, s_ref):
        head = work * PACK // blocks
        keys = [kv_ref[0, head] for kv_ref in kv_refs[slot]]
        s_ref[: half * len(keys)] = lax.dot_general(
            jnp.concatenate(keys, axis=0),
            q_ref[work],
            (((1,), (1,)), ((), ())),
            preferred_element_type=jnp.float32,
        )

    def finish(work, total):
        value = (total[:width] * (1.0 / total[width : width + 1])).astype(jnp.bfloat16)
        row = lax.broadcasted_iota(jnp.int32, (width, width), 0)
        column = lax.broadcasted_iota(jnp.int32, (width, width), 1)
        eye = jnp.where(row == column, 1.0, 0.0).astype(jnp.bfloat16)
        for piece in range(rows // width):
            cut = slice(piece * width, (piece + 1) * width)
            out_ref[work, cut] = lax.dot_general(
                eye, value[:, cut], (((1,), (1,)), ((), ())), preferred_element_type=jnp.float32
            ).astype(out_ref.dtype)

    def absorb(work, slot, s_ref, acc_src, top_src, final):
        head = work * PACK // blocks
        source = src_ref[units[slot][0]]
        offsets, values = [], []
        top = None
        for part, kv_ref in enumerate(kv_refs[slot]):
            base = source * blocks + (rep if units[slot][1][part] == 0 else 1 - rep) * half_blocks
            for piece in range(half_blocks):
                start = part * half + piece * block_rows
                offset = jnp.concatenate(
                    [
                        jnp.full((1, rows // PACK), bias_ref[work * PACK + index, base + piece])
                        for index in range(PACK)
                    ],
                    axis=1,
                )
                block = s_ref[start : start + block_rows]
                peak = jnp.max(block.reshape(block_rows // 8, 8, rows), axis=0) * scale + offset
                top = peak if top is None else jnp.maximum(top, peak)
                offsets.append(offset)
                values.append(kv_ref[1, head, piece * width : (piece + 1) * width, :])
        top = jnp.max(top, axis=0, keepdims=True)
        if acc_src is not None:
            before = top_src[work, :1]
            top = jnp.maximum(top, before)
        weights = []
        for index, offset in enumerate(offsets):
            block = s_ref[index * block_rows : (index + 1) * block_rows]
            weights.append(jnp.exp2(block * scale - (top - offset)).astype(jnp.bfloat16))
        value = jnp.concatenate(values, axis=1)
        ones = jnp.ones((ONES, value.shape[1]), value.dtype)
        value = jnp.concatenate([value, ones], axis=0)
        term = jnp.dot(
            value, jnp.concatenate(weights, axis=0), preferred_element_type=jnp.float32
        )[: width + KEEP]
        if acc_src is not None:
            term = term + acc_src[work] * jnp.exp2(before - top)
        if final:
            finish(work, term)
        else:
            acc_out[work] = term
            top_out[work] = jnp.broadcast_to(top, top_out.shape[1:])

    def sweep(slot, acc_src, top_src, final):
        score(0, slot, s_refs[0])

        @pl.loop(0, works // 2)
        def _(step):
            work = 2 * step
            score(work + 1, slot, s_refs[1])
            absorb(work, slot, s_refs[0], acc_src, top_src, final)
            score(jnp.minimum(work + 2, works - 1), slot, s_refs[0])
            absorb(work + 1, slot, s_refs[1], acc_src, top_src, final)

    if first:
        sweep(0, None, None, False)
        return
    valid = [src_ref[units[slot][0]] >= 0 for slot in range(slots)]
    seen = None
    for slot in range(slots):
        later = None
        for other in valid[slot + 1 :]:
            later = other if later is None else jnp.logical_or(later, other)
        starts = [(valid[slot], acc_in, top_in)]
        if seen is not None:
            starts = [
                (jnp.logical_and(valid[slot], jnp.logical_not(seen)), acc_in, top_in),
                (jnp.logical_and(valid[slot], seen), acc_out, top_out),
            ]
        for condition, acc_src, top_src in starts:
            if not last or later is None:
                pl.when(condition)(functools.partial(sweep, slot, acc_src, top_src, last))
            else:
                pl.when(jnp.logical_and(condition, later))(
                    functools.partial(sweep, slot, acc_src, top_src, False)
                )
                pl.when(jnp.logical_and(condition, jnp.logical_not(later)))(
                    functools.partial(sweep, slot, acc_src, top_src, True)
                )
        seen = valid[slot] if seen is None else jnp.logical_or(seen, valid[slot])

    @pl.when(jnp.logical_not(seen))
    def _():
        @pl.loop(0, works)
        def _(work):
            if last:
                finish(work, acc_in[work])
            else:
                acc_out[work] = acc_in[work]
                top_out[work] = top_in[work]


def attend_call(sources, bias, query, units, kv, state, last, scale):
    works, rows, width = query.shape
    first = state is None
    vmem = pl.BlockSpec(memory_space=pltpu.VMEM)
    smem = pl.BlockSpec(memory_space=pltpu.SMEM)
    operands = [sources, bias, query, *kv]
    specs = [smem, smem] + [vmem] * (1 + len(kv))
    shapes = [
        jax.ShapeDtypeStruct((works, width + KEEP, rows), jnp.float32),
        jax.ShapeDtypeStruct((works, KEEP, rows), jnp.float32),
    ]
    if not first:
        operands += list(state)
        specs += [vmem, vmem]
    if last:
        shapes = [jax.ShapeDtypeStruct((works, rows, width), jnp.bfloat16)] + shapes
    keys = max(len(parts) for _, parts in units) * kv[0].shape[2]
    work = works * rows * kv[0].shape[2] * len(kv)
    return pl.pallas_call(
        functools.partial(attend_kernel, units, kv[0].shape[1], first, last, scale),
        out_shape=shapes,
        in_specs=specs,
        out_specs=[vmem] * len(shapes),
        scratch_shapes=[pltpu.VMEM((keys, rows), jnp.float32)] * 2,
        compiler_params=pltpu.CompilerParams(vmem_limit_bytes=24 << 20),
        cost_estimate=pl.CostEstimate(
            flops=6 * work * width, bytes_accessed=4 * works * rows * width, transcendentals=work
        ),
    )(*operands)


def run(query_rows, key_rows, value_rows, dest_block, tile_list, tile_count, stripe_start):
    ctx_count = lax.axis_size("ctx")
    ctx_index = lax.axis_index("ctx")
    rep_index = lax.axis_index("rep")
    tok_rows, heads, group, width = query_rows.shape
    block_total = dest_block.shape[0]
    blocks = block_total // ctx_count
    block_rows = tok_rows // blocks
    half = tok_rows // 2
    scale = width ** (-0.5) * math.log2(math.e)

    def half_of(which):
        key_half = lax.dynamic_slice_in_dim(key_rows, which * half, half, 0)
        value_half = lax.dynamic_slice_in_dim(value_rows, which * half, half, 0)
        key_half = jnp.transpose(key_half, (1, 0, 2))
        value_half = value_half.reshape(half // block_rows, block_rows, heads, width)
        value_half = jnp.transpose(value_half, (2, 0, 3, 1)).reshape(key_half.shape)
        return jnp.stack([key_half, value_half])

    mine = half_of(rep_index)
    right = [(i, i + 1) for i in range(ctx_count - 1)]
    left = [(i + 1, i) for i in range(ctx_count - 1)]
    ends = [(0, ctx_count - 1), (ctx_count - 1, 0)]
    from_left = lax.ppermute(mine, "ctx", right)
    from_right = lax.ppermute(mine, "ctx", left)

    owner = dest_block // blocks
    stripes = jnp.sum(
        (stripe_start[:, :, None] // tok_rows == owner[None, None, :]).astype(jnp.int32), axis=1
    )
    placed = lax.dynamic_slice_in_dim(dest_block, ctx_index * blocks, blocks, 0)
    row_pick = (placed[:, None] == jnp.arange(block_total)[None, :]).astype(jnp.int32)
    used = jnp.arange(tile_list.shape[1])[None, :] < tile_count[:, None]
    listed = jnp.sum(
        (used[:, :, None] & (tile_list[:, :, None] == dest_block[None, None, :])).astype(jnp.int32),
        axis=1,
    )
    near = jnp.sum(row_pick[:, :, None] * listed[None], axis=1)
    count = stripes[:, None, :] + near[None, :, :]
    bias = jnp.where(count > 0, jnp.log2(jnp.maximum(count, 1).astype(jnp.float32)), NEG)
    bias = bias.reshape(heads * blocks, block_total)

    query = query_rows.reshape(blocks, block_rows, heads, group, width)
    query = jnp.transpose(query, (2, 0, 3, 1, 4)).reshape(
        heads * blocks // PACK, PACK * group * block_rows, width
    )

    is_end = (ctx_index == 0) | (ctx_index == ctx_count - 1)
    opposite = jnp.where(ctx_index == 0, ctx_count - 1, 0)
    sources = [rep_index, ctx_index, jnp.where(is_end, opposite, -1)]
    for hop in range(1, ctx_count):
        sources.append(ctx_index - hop)
        sources.append(jnp.where(ctx_index + hop < ctx_count, ctx_index + hop, -1))
    sources = jnp.stack(sources).astype(jnp.int32)

    def call(units, kv, state, last=False):
        return attend_call(sources, bias, query, units, kv, state, last, scale)

    def swap(array):
        return lax.ppermute(array, "rep", [(0, 1), (1, 0)])

    both = (0, 1)
    state = call(((1, both),), (mine, half_of(1 - rep_index)), None)
    if ctx_count > 2:
        far = lax.ppermute(mine, "ctx", ends)
    final_hop = max(1, ctx_count - 2)
    for hop in range(1, final_hop + 1):
        here_left, here_right = from_left, from_right
        if hop < final_hop:
            from_left = lax.ppermute(here_left, "ctx", right)
            from_right = lax.ppermute(here_right, "ctx", left)
        elif ctx_count > 2:
            state = call(((2, both),), (far, swap(far)), state)
        slot = 1 + 2 * hop
        there_left = swap(here_left)
        there_right = swap(here_right)
        if hop < final_hop:
            kv = (here_left, there_left, here_right, there_right)
            state = call(((slot, both), (slot + 1, both)), kv, state)
        else:
            kv = (here_left, there_left, here_right, there_right)
            state = call(((slot, both), (slot + 1, both)), kv, state, True)
    out = state[0]
    out = out.reshape(heads, blocks, group, block_rows, width)
    return jnp.transpose(out, (1, 3, 0, 2, 4)).reshape(query_rows.shape)


def solution(mesh):
    in_specs = (
        P(("parts", "ctx"), "head", "rep", None),
        P(("parts", "ctx"), "head", None),
        P(("parts", "ctx"), "head", None),
        P("parts"),
        P("parts", None),
        P("parts"),
        P(("parts", "head"), None),
    )
    out_specs = P(("parts", "ctx"), "head", "rep", None)
    return jax.shard_map(run, mesh=mesh, in_specs=in_specs, out_specs=out_specs, check_vma=False)
```
